32 devices in a mesh: seq: 8 (over y, x, core), weight: 4 (over z).
Axes of the slice: x: 2, y: 2, z: 4, core: 2. Of those that a mesh axis runs over, the one named last changes fastest.
Arguments:
- tokens: bfloat16 [4, 4096, 1024], P('weight', 'seq'), may hold values from -6 to 6
- cotangent: bfloat16 [4, 4096, 1024], P('weight', 'seq'), may hold values from -6 to 6
- offsets: int32 [4, 3], P('weight'), may hold values from 0 to 4096, as said below
- qkv_weight: bfloat16 [2, 1024, 3072], P(None, 'weight'), may hold values from -0.1875 to 0.1875
- attn_out_weight: bfloat16 [2, 1024, 1024], P(None, 'weight'), may hold values from -0.75 to 0.75
- mlp_in_weight: bfloat16 [2, 1024, 5248], P(None, 'weight'), may hold values from -0.1875 to 0.1875
- mlp_out_weight: bfloat16 [2, 2624, 1024], P(None, None, 'weight'), may hold values from -0.125 to 0.125
- norm_gains: bfloat16 [2, 2, 1024], P(None, None, 'weight'), may hold values from 0.5 to 1.5
Outputs:
- output: bfloat16 [4, 4096, 1024], P('weight', 'seq')
- input_grad: float32 [4, 4096, 1024], P('weight', 'seq')
- grad_qkv: float32 [2, 1024, 3072], P(None, 'weight')
- grad_attn_out: float32 [2, 1024, 1024], P(None, 'weight')
- grad_mlp_in: float32 [2, 1024, 5248], P(None, 'weight')
- grad_mlp_out: float32 [2, 2624, 1024], P(None, None, 'weight')
- grad_gains: float32 [2, 2, 1024], P(None, None, 'weight')
The draws below stay inside these ranges and needn't reach their ends.
Inputs may be any that keep to these rules, and one draw needn't show every extreme that they name: offsets[g] = (0, c, 4096): a group holds two sequences, tokens 0 to c - 1 and c to 4095, with c from 1024 to 3072.
All inputs are finite; a program needn't handle non-finite values.
Results may differ from the reference program's by a relative error of at most 0.025.
Values may be sent and summed in bfloat16 or wider, within the bound.
No kernel may reach another device: no remote copies, remote signals or barrier semaphores. Data moves between devices by JAX's collectives and lax.ppermute only.
A program may use at most 384 MiB of HBM per device.

```python
import jax
import jax.numpy as jnp
from jax import lax

D = 1024
HEADS = 16
HEAD_DIM = 64
FF = 2624
HALF = 64
LAYERS = 2
TOK_DEV = 512
GROUPS = 4
SEQ_TOK = 4096


def draw_offsets(key, part):
    cut = jax.random.randint(key, (GROUPS,), SEQ_TOK // 4, 3 * SEQ_TOK // 4 + 1).astype(jnp.int32)
    zeros = jnp.zeros((GROUPS,), jnp.int32)
    ending = jnp.full((GROUPS,), SEQ_TOK, jnp.int32)
    return jnp.stack([zeros, cut, ending], axis=1).astype(jnp.int32)


def spiked(entries, rng, source, target, shards_of, factor):
    owner, partner = [(jnp.arange(entries.shape[dim]) // (entries.shape[dim] // shards_of)).reshape([-1 if axis == dim else 1 for axis in range(entries.ndim)]) for dim in (source, target)]
    chosen = jax.random.permutation(rng, shards_of)[partner]
    strong = (owner == chosen) | (owner == (partner + shards_of // 2) % shards_of)
    return jnp.where(strong, factor * entries, entries)


def steps_of(stream_key, extent, shards, low, top_value):
    def one(dim, shards_of):
        steps = jax.random.uniform(jax.random.fold_in(jax.random.fold_in(stream_key, 6), dim), (shards_of,), jnp.float32, low / len(shards), top_value / len(shards))
        return jnp.repeat(jnp.exp(steps), extent[dim] // shards_of).reshape((-1,) + (1,) * (len(extent) - dim - 1))

    level = one(*shards[0])
    for cut in shards[1:]:
        level = level * one(*cut)
    return level


def noise(own_key, dims, scale, bound, pieces=(), kind=jnp.bfloat16):
    loudness = steps_of(own_key, dims, pieces, -0.22, 0.18) if pieces else 1.0
    entries = jax.random.normal(own_key, dims, jnp.float32) * scale * loudness
    return jnp.minimum(jnp.maximum(entries, -bound), bound).astype(kind)


def gaussian_with(stream_key, shape, deviation, bound, pieces, heavy, kind=jnp.bfloat16):
    array = deviation * jax.random.normal(stream_key, shape, jnp.float32)
    if pieces:
        array = array * steps_of(stream_key, shape, pieces, -0.22, 0.18)
    return jnp.clip(spiked(array, jax.random.fold_in(stream_key, 3), *heavy), -bound, bound).astype(kind)


def setup_inputs(seed: int = 0) -> dict:
    key_list = jax.random.split(jax.random.key(seed), 9)
    return {
        "tokens": noise(key_list[0], (GROUPS, SEQ_TOK, D), 1.0, 6.0, ((0, 4), (1, 8))),
        "cotangent": gaussian_with(key_list[1], (GROUPS, SEQ_TOK, D), 1.0, 6.0, ((0, 4), (1, 8)), (1, 2, 8, 2.0)),
        "offsets": draw_offsets(jax.random.fold_in(key_list[8], 71), 0),
        "qkv_weight": noise(key_list[3], (LAYERS, D, 3 * D), D ** -0.5, 0.1875, ((1, 4),)),
        "attn_out_weight": noise(key_list[4], (LAYERS, D, D), (D // 16) ** -0.5, 0.75, ((1, 4),)),
        "mlp_in_weight": noise(key_list[5], (LAYERS, D, 2 * FF), D ** -0.5, 0.1875, ((1, 4),)),
        "mlp_out_weight": noise(key_list[6], (LAYERS, FF, D), FF ** -0.5, 0.125, ((2, 4),)),
        "norm_gains": jnp.clip(1.0 + 0.1 * jax.random.normal(key_list[7], (LAYERS, 2, D), jnp.float32), 0.5, 1.5).astype(jnp.bfloat16),
    }


EPS = 1e-05
THETA = 10000.0
NEG = -1e+30
HIGH = lax.Precision.HIGHEST

@jax.custom_vjp
def low(v):
    return lax.optimization_barrier(v.astype(jnp.bfloat16)).astype(jnp.float32)

@jax.custom_vjp
def low_back(v):
    return v

def low_keep(v):
    return (low(v), None)

def low_pass(kept, grad):
    return (grad,)

def back_keep(v):
    return (v, None)

def back_low(kept, grad):
    return (low(grad),)
low.defvjp(low_keep, low_pass)
low_back.defvjp(back_keep, back_low)

def layer_norm(values, gain):
    center = values - lax.optimization_barrier(jnp.mean(values, axis=-1, keepdims=True))
    spread = lax.optimization_barrier(jnp.mean(center * center, axis=-1, keepdims=True))
    return center * lax.rsqrt(spread + EPS) * gain

def seq_start(places, bounds):
    return jnp.where(places >= bounds[1], bounds[1], 0).astype(jnp.int32)

def rotate(values, places):
    half = HEAD_DIM // 2
    freq = THETA ** (-2.0 * jnp.arange(half, dtype=jnp.float32) / HEAD_DIM)
    angle = places.astype(jnp.float32)[:, None] * freq[None, :]
    cosine = jnp.concatenate([jnp.cos(angle), jnp.cos(angle)], axis=1)[:, None, :]
    sine = jnp.concatenate([jnp.sin(angle), jnp.sin(angle)], axis=1)[:, None, :]
    heads = values.reshape(values.shape[0], HEADS, HEAD_DIM)
    turned = jnp.concatenate([-heads[..., half:], heads[..., :half]], axis=-1)
    return (heads * cosine + turned * sine).reshape(values.shape)

def window_mask(query_glob, key_glob, bounds, total_rows):
    near = jnp.abs(query_glob[:, None] - key_glob[None, :]) <= HALF
    inside = (key_glob >= 0) & (key_glob < total_rows)
    same = seq_start(query_glob, bounds)[:, None] == seq_start(key_glob, bounds)[None, :]
    return near & inside[None, :] & same

def attention(queries, keys, values, bounds):
    key_pad = jnp.pad(keys, ((HALF, HALF), (0, 0)))
    value_pad = jnp.pad(values, ((HALF, HALF), (0, 0)))
    blocks = SEQ_TOK // TOK_DEV

    def one_block(block_idx):
        first_row = (block_idx * TOK_DEV).astype(jnp.int32)
        query_blk = lax.dynamic_slice_in_dim(queries, first_row, TOK_DEV, 0)
        key_blk = lax.dynamic_slice_in_dim(key_pad, first_row, TOK_DEV + 2 * HALF, 0)
        value_blk = lax.dynamic_slice_in_dim(value_pad, first_row, TOK_DEV + 2 * HALF, 0)
        query_glob = first_row + jnp.arange(TOK_DEV, dtype=jnp.int32)
        key_glob = first_row - HALF + jnp.arange(TOK_DEV + 2 * HALF, dtype=jnp.int32)
        window = window_mask(query_glob, key_glob, bounds, SEQ_TOK)
        query_heads = query_blk.reshape(TOK_DEV, HEADS, HEAD_DIM)
        key_heads = key_blk.reshape(-1, HEADS, HEAD_DIM)
        value_heads = value_blk.reshape(-1, HEADS, HEAD_DIM)
        raw = jnp.einsum('qhd,khd->hqk', query_heads, key_heads, precision=HIGH) * HEAD_DIM ** (-0.5)
        raw = low_back(raw)
        scores = jnp.where(window[None], raw, NEG)
        top = lax.optimization_barrier(jnp.max(scores, axis=-1, keepdims=True))
        log_total = top + jnp.log(lax.optimization_barrier(jnp.sum(jnp.exp(scores - top), axis=-1, keepdims=True)))
        prob = jnp.exp(scores - log_total)
        result = jnp.einsum('hqk,khd->qhd', low(prob), value_heads, precision=HIGH)
        return result.reshape(TOK_DEV, HEADS * HEAD_DIM)
    outputs = lax.map(jax.checkpoint(one_block), jnp.arange(blocks, dtype=jnp.int32))
    return outputs.reshape(SEQ_TOK, HEADS * HEAD_DIM)

def layer_block(stream, weights, places, bounds):
    w_qkv, w_attn, w_in, w_out, gain = weights
    normed = low(layer_norm(stream, gain[0]))
    mixed = low_back(jnp.dot(normed, w_qkv, precision=HIGH))
    queries = low(rotate(mixed[:, :D], places))
    keys = low(rotate(mixed[:, D:2 * D], places))
    values = low(mixed[:, 2 * D:])
    context = low(low_back(attention(queries, keys, values, bounds)))
    middle = stream + low_back(jnp.dot(context, w_attn, precision=HIGH))
    shaped = low(layer_norm(middle, gain[1]))
    gate_up = low_back(jnp.dot(shaped, w_in, precision=HIGH))
    hidden = low(jax.nn.gelu(gate_up[:, :FF], approximate=False) * gate_up[:, FF:])
    return middle + low_back(jnp.dot(hidden, w_out, precision=HIGH))

def reference(tokens, cotangent, offsets, qkv_weight, attn_out_weight, mlp_in_weight, mlp_out_weight, norm_gains):
    params = tuple((member.astype(jnp.float32) for member in (qkv_weight, attn_out_weight, mlp_in_weight, mlp_out_weight, norm_gains)))

    def group_step(carry, items):
        group_tokens, group_cot, bounds = items
        positions = jnp.arange(SEQ_TOK, dtype=jnp.int32)
        places = positions - seq_start(positions, bounds)

        def forward(stream, *weights):
            for layer_idx in range(LAYERS):
                stream = layer_block(stream, tuple((member[layer_idx] for member in weights)), places, bounds)
            return stream
        result, pull = jax.vjp(forward, group_tokens.astype(jnp.float32), *params)
        grads = pull(group_cot.astype(jnp.float32))
        updated = tuple((total + part for total, part in zip(carry, grads[1:])))
        return (updated, (result.astype(jnp.bfloat16), grads[0]))
    start_sums = tuple((jnp.zeros(member.shape, jnp.float32) for member in params))
    sums, (outputs, input_grad) = lax.scan(group_step, start_sums, (tokens, cotangent, offsets))
    return (outputs, input_grad, sums[0], sums[1], sums[2], sums[3], sums[4])
```

```python
import jax
import jax.numpy as jnp
from jax import lax
from jax.experimental import pallas as pl
from jax.experimental.pallas import tpu as pltpu
from jax.sharding import PartitionSpec as P

HEADS = 16
HEAD_DIM = 64
HALF = 64


EPS = 1e-05
THETA = 10000.0
NEG = -1e30


def padded(cells, sides, width):
    for axis, dim in sides:
        count = lax.axis_size(axis)
        ends = count - 1
        head = lax.slice_in_dim(cells, 0, width, axis=dim)
        tail = lax.slice_in_dim(cells, cells.shape[dim] - width, cells.shape[dim], axis=dim)
        cells = jnp.concatenate(
            [
                lax.ppermute(tail, axis, [(i, (i + 1) % count) for i in range(ends)]),
                cells,
                lax.ppermute(head, axis, [((i + 1) % count, i) for i in range(ends)]),
            ],
            axis=dim,
        )
    return cells


def layer_norm(values, gain):
    center = values - jnp.mean(values, axis=-1, keepdims=True)
    spread = jnp.mean(center * center, axis=-1, keepdims=True)
    return center * lax.rsqrt(spread + EPS) * gain


def seq_start(places, bounds):
    return jnp.where(places >= bounds[1], bounds[1], 0)


def rotate(values, places):
    half = HEAD_DIM // 2
    freq = THETA ** (-2.0 * jnp.arange(half, dtype=jnp.float32) / HEAD_DIM)
    angle = places.astype(jnp.float32)[:, None] * freq[None, :]
    cosine = jnp.concatenate([jnp.cos(angle), jnp.cos(angle)], axis=1)[:, None, :]
    sine = jnp.concatenate([jnp.sin(angle), jnp.sin(angle)], axis=1)[:, None, :]
    heads = values.reshape(values.shape[0], HEADS, HEAD_DIM)
    turned = jnp.concatenate([-heads[..., half:], heads[..., :half]], axis=-1)
    return (heads * cosine + turned * sine).reshape(values.shape)


def window_mask(query_glob, key_glob, bounds, total_rows):
    near = jnp.abs(query_glob[:, None] - key_glob[None, :]) <= HALF
    inside = (key_glob >= 0) & (key_glob < total_rows)
    same = seq_start(query_glob, bounds)[:, None] == seq_start(key_glob, bounds)[None, :]
    return near & inside[None, :] & same


def geglu(gate_up):
    width = gate_up.shape[1] // 2
    return jax.nn.gelu(gate_up[:, :width], approximate=False) * gate_up[:, width:]


def inner(left, right):
    return lax.dot_general(
        left, right, (((0,), (0,)), ((), ())), preferred_element_type=jnp.float32
    )


def outer(left, right):
    return lax.dot_general(
        left, right, (((1,), (1,)), ((), ())), preferred_element_type=jnp.float32
    )


def split_heads(values):
    return values.reshape(values.shape[0], HEADS, HEAD_DIM)


def attn_scores(queries, key_wide, window):
    raw = jnp.einsum(
        "qhd,khd->hqk",
        split_heads(queries),
        split_heads(key_wide),
        preferred_element_type=jnp.float32,
    )
    return jnp.where(window[None], raw * HEAD_DIM ** (-0.5), NEG)


LANES = 128


def pad_lanes(values):
    extra = -values.shape[-1] % LANES
    return jnp.pad(values, ((0, 0),) * (values.ndim - 1) + ((0, extra),))


def seq_swap(values, bit):
    count = lax.axis_size("seq")
    return lax.ppermute(values, "seq", [(i, i ^ bit) for i in range(count)])


def chip_orders(pieces):
    bits = [1 << k for k in range(1, lax.axis_size("seq").bit_length() - 1)]
    return [bits[p % len(bits) :] + bits[: p % len(bits)] for p in range(pieces)]


def part_bounds(total, parts):
    edges = [total * p // parts for p in range(parts + 1)]
    return list(zip(edges[:-1], edges[1:]))


def spread(part, order):
    held = {0: part}
    for bit in order:
        held.update({mask ^ bit: seq_swap(piece, bit) for mask, piece in list(held.items())})
    return held


def assemble_kernel(index_ref, *refs, plan, count_in, count_out):
    sources = refs[:count_in]
    targets = refs[count_in : count_in + count_out]
    sems = refs[-1]
    index = index_ref[0]
    copies = []
    for number, (mask, low, high) in enumerate(plan):
        place = jnp.bitwise_xor(index, mask)
        column = 0
        for which, target in enumerate(targets):
            wide = target.shape[-1]
            copies.append(
                pltpu.make_async_copy(
                    sources[number].at[:, :, column : column + wide],
                    target.at[low:high, place],
                    sems.at[number, which],
                )
            )
            column += wide
    for copy in copies:
        copy.start()
    for copy in copies:
        copy.wait()


def assemble(index, parts, widths):
    count = lax.axis_size("seq")
    plan, sources = [], []
    for low, high, held in parts:
        for mask, piece in held.items():
            plan.append((mask, low, high))
            sources.append(piece)
    lead = parts[-1][1]
    rows = sources[0].shape[1]
    kind = sources[0].dtype

    def kernel(*refs):
        assemble_kernel(*refs, plan=plan, count_in=len(sources), count_out=len(widths))

    anywhere = pl.BlockSpec(memory_space=pl.ANY)
    return pl.pallas_call(
        kernel,
        out_shape=[jax.ShapeDtypeStruct((lead, count, rows, wide), kind) for wide in widths],
        grid_spec=pltpu.PrefetchScalarGridSpec(
            num_scalar_prefetch=1,
            grid=(),
            in_specs=[anywhere] * len(sources),
            out_specs=[pl.BlockSpec(memory_space=pltpu.VMEM)] * len(widths),
            scratch_shapes=[pltpu.SemaphoreType.DMA((len(plan), len(widths)))],
        ),
        name="assemble",
    )(index.reshape(1), *sources)


def line_up(columns):
    index = lax.axis_index("seq")
    rows = columns[0].shape[0] // lax.axis_size("seq")
    own = jnp.concatenate(
        [lax.dynamic_slice_in_dim(member, index * rows, rows, 0) for member in columns], axis=1
    )
    return lax.all_gather(own, "weight", axis=0, tiled=False)


def fill_out(line, widths):
    groups, rows, _ = line.shape
    count = lax.axis_size("seq")
    orders = chip_orders(min(groups, max(1, count.bit_length() - 2)))
    parts = [
        (low, high, spread(line[low:high], order + [1]))
        for (low, high), order in zip(part_bounds(groups, len(orders)), orders)
    ]
    whole = assemble(lax.axis_index("seq"), parts, widths)
    return [member.reshape(groups * count * rows, -1) for member in whole]


def fetch_start(pieces):
    w_qkv, w_attn, w_in, w_out, gain_low = pieces
    width = w_in.shape[1] // 2
    first = [w_qkv, w_attn, pad_lanes(gain_low.T)]
    second = [
        jnp.concatenate([pad_lanes(w_in[:, :width]), pad_lanes(w_in[:, width:])], axis=1),
        pad_lanes(w_out.T),
    ]
    return tuple((line_up(some), [member.shape[1] for member in some]) for some in (first, second))


def fetch_first(line, widths):
    full_qkv, full_attn, full_gain = fill_out(line, widths)
    return full_qkv, full_attn, full_gain[:, :2].T


def fetch_second(line, widths):
    return tuple(fill_out(line, widths))


def sum_grads(members):
    index = lax.axis_index("seq")
    count = lax.axis_size("seq")
    groups = lax.axis_size("weight")
    rows = members[0].shape[0] // (count * groups)
    bits = count.bit_length() - 2

    def side(bit):
        return (index // bit) % 2

    def half(values, axis, which):
        return lax.dynamic_index_in_dim(values, which, axis, keepdims=False)

    split = [m.reshape((groups,) + (2,) * (bits + 1) + (rows, m.shape[1])) for m in members]
    send = jnp.concatenate([half(m, bits + 1, 1 - side(1)) for m in split], axis=-1)
    keep = jnp.concatenate([half(m, bits + 1, side(1)) for m in split], axis=-1)
    got = yield seq_swap(send, 1)
    total = keep + got
    orders = chip_orders(min(groups, max(1, bits)))
    bounds = part_bounds(groups, len(orders))
    parts = [total[low:high] for low, high in bounds]
    left = [[1 << k for k in range(bits, 0, -1)] for _ in parts]
    for step in range(bits):
        axes = [1 + rest.index(order[step]) for rest, order in zip(left, orders)]
        for rest, order in zip(left, orders):
            rest.remove(order[step])
        got = yield [
            seq_swap(half(part, axis, 1 - side(order[step])), order[step])
            for part, axis, order in zip(parts, axes, orders)
        ]
        parts = [
            half(part, axis, side(order[step])) + more
            for part, axis, order, more in zip(parts, axes, orders, got)
        ]
    line = jnp.concatenate(parts, axis=0).reshape(groups * rows, -1)
    own = lax.psum_scatter(line, "weight", scatter_dimension=0, tiled=True)
    yield None
    own = yield own
    held = {0: own[None]}
    for bit in chip_orders(1)[0] + [1]:
        masks = list(held)
        got = yield [seq_swap(held[mask], bit) for mask in masks]
        held.update({mask ^ bit: more for mask, more in zip(masks, got)})
    whole = assemble(index, [(0, 1, held)], [m.shape[1] for m in members])
    return [m.reshape(count * rows, -1) for m in whole]


class Sums:
    def __init__(self):
        self.active = []
        self.done = {}

    def add(self, key, members):
        chain = sum_grads(members)
        self.active.append((key, chain, next(chain)))

    def step(self, flights):
        after = []
        for (key, chain, _), flight in zip(self.active, flights):
            try:
                after.append((key, chain, chain.send(flight)))
            except StopIteration as end:
                self.done[key] = end.value
        self.active = after

    def tie(self, value):
        value, flights = lax.optimization_barrier((value, [entry[2] for entry in self.active]))
        self.step(flights)
        return value

    def finish(self):
        while self.active:
            self.step([entry[2] for entry in self.active])


def layer_forward(stream, lines, ahead, places, window):
    (first_line, first_widths), (second_line, second_widths) = lines
    w_qkv, w_attn, gain_low = fetch_first(first_line, first_widths)
    w_in, w_out = fetch_second(second_line, second_widths)
    next_lines = None
    gain = gain_low.astype(jnp.float32)
    width = stream.shape[1]
    normed = layer_norm(stream, gain[0]).astype(jnp.bfloat16)
    mixed = jnp.dot(normed, w_qkv, preferred_element_type=jnp.float32)
    if ahead is not None:
        (next_first, widths_one), (next_second, widths_two) = ahead
        mixed, next_first = lax.optimization_barrier((mixed, next_first))
    queries = rotate(mixed[:, :width], places).astype(jnp.bfloat16)
    keys = rotate(mixed[:, width : 2 * width], places).astype(jnp.bfloat16)
    values = mixed[:, 2 * width :].astype(jnp.bfloat16)
    kv_wide = padded(jnp.concatenate([keys, values], axis=1), (("seq", 0),), HALF)
    scores = attn_scores(queries, kv_wide[:, :width], window)
    top = jnp.max(scores, axis=-1, keepdims=True)
    log_total = top + jnp.log(jnp.sum(jnp.exp(scores - top), axis=-1, keepdims=True))
    prob = jnp.exp(scores - log_total).astype(jnp.bfloat16)
    context = jnp.einsum(
        "hqk,khd->qhd", prob, split_heads(kv_wide[:, width:]), preferred_element_type=jnp.float32
    )
    context = context.reshape(stream.shape).astype(jnp.bfloat16)
    if ahead is not None:
        context, next_second = lax.optimization_barrier((context, next_second))
        next_lines = ((next_first, widths_one), (next_second, widths_two))
    middle = stream + jnp.dot(context, w_attn, preferred_element_type=jnp.float32)
    shaped = layer_norm(middle, gain[1]).astype(jnp.bfloat16)
    gate_up = jnp.dot(shaped, w_in, preferred_element_type=jnp.float32)
    hidden = geglu(gate_up).astype(jnp.bfloat16)
    result = middle + outer(hidden, w_out)
    return (
        result,
        next_lines,
        (w_qkv, w_attn, w_in, w_out, gain_low),
        (stream, normed, queries, kv_wide, log_total, context, middle, shaped, gate_up, hidden),
    )


def layer_backward(upstream, weights, saved_acts, places, window, sums, layer_idx):
    w_qkv, w_attn, w_in, w_out, gain_low = weights
    gain = gain_low.astype(jnp.float32)
    stream, normed, queries, kv_wide, log_total, context, middle, shaped, gate_up, hidden = (
        saved_acts
    )
    width = stream.shape[1]
    rows_here = stream.shape[0]
    up_low = upstream.astype(jnp.bfloat16)
    grad_out = inner(up_low, hidden).astype(jnp.bfloat16)
    sums.add((layer_idx, "out"), [grad_out])
    d_hidden = jnp.dot(up_low, w_out, preferred_element_type=jnp.float32)
    d_gate_up = jax.vjp(geglu, gate_up)[1](d_hidden)[0].astype(jnp.bfloat16)
    d_gate_up = sums.tie(d_gate_up)
    grad_in = inner(shaped, d_gate_up).astype(jnp.bfloat16)
    sums.add((layer_idx, "in"), [grad_in])
    d_shaped = outer(d_gate_up, w_in)
    mid_part, gain_two = jax.vjp(layer_norm, middle, gain[1])[1](d_shaped)
    d_middle = sums.tie(upstream + mid_part)
    mid_low = d_middle.astype(jnp.bfloat16)
    grad_attn = inner(context, mid_low).astype(jnp.bfloat16)
    d_context = sums.tie(outer(mid_low, w_attn).astype(jnp.bfloat16))
    key_wide = kv_wide[:, :width]
    value_wide = kv_wide[:, width:]
    prob = jnp.exp(attn_scores(queries, key_wide, window) - log_total)
    context_heads = split_heads(d_context)
    d_prob = jnp.einsum(
        "qhd,khd->hqk", context_heads, split_heads(value_wide), preferred_element_type=jnp.float32
    )
    delta = jnp.sum(prob * d_prob, axis=-1, keepdims=True)
    d_score = (prob * (d_prob - delta)).astype(jnp.bfloat16)
    scale = HEAD_DIM ** (-0.5)
    d_query = (
        jnp.einsum(
            "hqk,khd->qhd", d_score, split_heads(key_wide), preferred_element_type=jnp.float32
        )
        * scale
    )
    d_key = (
        jnp.einsum(
            "hqk,qhd->khd", d_score, split_heads(queries), preferred_element_type=jnp.float32
        )
        * scale
    )
    d_value = jnp.einsum(
        "hqk,qhd->khd", prob.astype(jnp.bfloat16), context_heads, preferred_element_type=jnp.float32
    )
    d_key, d_value = sums.tie((d_key, d_value))
    d_kv = jnp.concatenate(
        [d_key.reshape(key_wide.shape), d_value.reshape(value_wide.shape)], axis=1
    )
    rims = jnp.concatenate([d_kv[:HALF], d_kv[-HALF:]], axis=0)
    returned = padded(rims.astype(jnp.bfloat16), (("seq", 0),), HALF).astype(rims.dtype)
    own_grad = d_kv[HALF : HALF + rows_here]
    own_grad = own_grad + jnp.pad(returned[:HALF], ((0, rows_here - HALF), (0, 0)))
    own_grad = own_grad + jnp.pad(returned[-HALF:], ((rows_here - HALF, 0), (0, 0)))
    d_mixed = jnp.concatenate(
        [
            rotate(d_query.reshape(stream.shape), -places),
            rotate(own_grad[:, :width], -places),
            own_grad[:, width:],
        ],
        axis=1,
    ).astype(jnp.bfloat16)
    d_mixed = sums.tie(d_mixed)
    grad_qkv = inner(normed, d_mixed).astype(jnp.bfloat16)
    d_normed = outer(d_mixed, w_qkv)
    in_part, gain_one = jax.vjp(layer_norm, stream, gain[0])[1](d_normed)
    d_stream = d_middle + in_part
    grad_gain = pad_lanes(jnp.stack([gain_one, gain_two], axis=1)).astype(jnp.bfloat16)
    sums.add((layer_idx, "rest"), [grad_qkv, grad_attn, grad_gain])
    if layer_idx:
        d_stream = sums.tie(d_stream)
    return d_stream


def body(
    tokens,
    cotangent,
    offsets,
    qkv_weight,
    attn_out_weight,
    mlp_in_weight,
    mlp_out_weight,
    norm_gains,
):
    layer_count = qkv_weight.shape[0]
    stream = tokens[0].astype(jnp.float32)
    bounds = offsets[0]
    rows_here = stream.shape[0]
    first_row = lax.axis_index("seq") * rows_here
    total_rows = lax.axis_size("seq") * rows_here
    query_glob = first_row + jnp.arange(rows_here, dtype=jnp.int32)
    key_glob = first_row - HALF + jnp.arange(rows_here + 2 * HALF, dtype=jnp.int32)
    places = query_glob - seq_start(query_glob, bounds)
    window = window_mask(query_glob, key_glob, bounds, total_rows)

    def pick(layer_idx):
        return (
            qkv_weight[layer_idx],
            attn_out_weight[layer_idx],
            mlp_in_weight[layer_idx],
            mlp_out_weight[layer_idx],
            norm_gains[layer_idx],
        )

    kept_weights = []
    saved_list = []
    lines = [fetch_start(pick(layer_idx)) for layer_idx in range(layer_count)]
    ready = lines[0]
    for layer_idx in range(layer_count):
        ahead = lines[layer_idx + 1] if layer_idx + 1 < layer_count else None
        stream, ready, weights, cache = layer_forward(stream, ready, ahead, places, window)
        kept_weights.append(weights)
        saved_list.append(cache)
    output = stream.astype(jnp.bfloat16)[None]
    upstream = cotangent[0].astype(jnp.float32)
    sums = Sums()
    for layer_idx in reversed(range(layer_count)):
        upstream = layer_backward(
            upstream,
            kept_weights[layer_idx],
            saved_list[layer_idx],
            places,
            window,
            sums,
            layer_idx,
        )
    sums.finish()
    results = []
    for layer_idx in range(layer_count):
        (sum_out,), (sum_in,) = sums.done[layer_idx, "out"], sums.done[layer_idx, "in"]
        sum_qkv, sum_attn, sum_gain = sums.done[layer_idx, "rest"]
        results.append((sum_qkv, sum_attn, sum_in, sum_out, sum_gain))
    hidden_width = mlp_in_weight.shape[2] // 2
    padded_width = hidden_width + -hidden_width % LANES

    def finish(member):
        return jnp.stack([results[layer_idx][member] for layer_idx in range(layer_count)])

    sum_in = finish(2)
    return (
        output,
        upstream[None],
        finish(0).astype(jnp.float32),
        finish(1).astype(jnp.float32),
        jnp.concatenate(
            [sum_in[..., :hidden_width], sum_in[..., padded_width : padded_width + hidden_width]],
            axis=2,
        ).astype(jnp.float32),
        jnp.swapaxes(finish(3)[..., :hidden_width], 1, 2).astype(jnp.float32),
        jnp.swapaxes(finish(4)[..., :2], 1, 2).astype(jnp.float32),
    )


def solution(mesh):
    return jax.shard_map(
        body,
        mesh=mesh,
        in_specs=(
            P("weight", "seq", None),
            P("weight", "seq", None),
            P("weight", None),
            P(None, "weight", None),
            P(None, "weight", None),
            P(None, "weight", None),
            P(None, None, "weight"),
            P(None, None, "weight"),
        ),
        out_specs=(
            P("weight", "seq", None),
            P("weight", "seq", None),
            P(None, "weight", None),
            P(None, "weight", None),
            P(None, "weight", None),
            P(None, None, "weight"),
            P(None, None, "weight"),
        ),
        check_vma=False,
    )
```
